32 devices in a mesh: grp: 2 (over x), region: 8 (over z, y), donor: 2 (over core).
Axes of the slice: x: 2, y: 2, z: 4, core: 2. Of those that a mesh axis runs over, the one named last changes fastest.
Arguments:
- dosage: bfloat16 [16384, 8192], P(('grp', 'region'), 'donor'), parts along dimension 0, may hold values from 0 to 2, as said below
- expression: bfloat16 [512, 8192], P(('grp', 'region'), 'donor'), parts along dimension 0, may hold values from -60 to 60
- cis_tiles: int32 [512, 8], P(('grp', 'region')), parts along dimension 0, may hold values from 0 to 63, as said below
Outputs:
- correlation: float32 [512, 1024], P(('grp', 'region'), 'donor'), parts along dimension 0
- pvalue: float32 [512, 1024], P(('grp', 'region'), 'donor'), parts along dimension 0
The draws below stay inside these ranges and needn't reach their ends.
There are 2 independent parts, one for each index of `grp`. The reference program is written for one: setup_inputs(seed, part) draws one part's arguments, and reference() takes and returns one part's arrays. A program takes and returns all parts, laid end to end along the dimension named above; each array names one. Nothing has to cross between parts.
Inputs may be any that keep to these rules, and one draw needn't show every extreme that they name: `dosage`: imputed dosages, within the bounds. `cis_tiles`: each gene's 8 cis tiles are consecutive tile numbers; for the genes of region block r (rows r * 32 to (r + 1) * 32 - 1) they lie from r * 8 - 8 to (r + 1) * 8 + 7, and both ends are reached in every block where they exist.
All inputs are finite; a program needn't handle non-finite values.
Results may differ from the reference program's by a relative error of at most 0.0044.
Values may be sent and summed in bfloat16 or wider, within the bound.
A program may use at most 128 MiB of HBM per device.

```python
import math
import jax
import jax.numpy as jnp
from jax import lax

DONORS = 8192
TILE = 128
VT_DEV = 8
VTILES = 64
VARIANTS = 8192
G_DEV = 32
GENES = 256
K = 8
RIM = 8
CF_TERMS = 32


def dose_rows(key, variant_ids):
    base_key = jax.random.fold_in(key, 11)

    def single_row(variant):
        row_key = jax.random.fold_in(base_key, variant)
        freq_key, noise_key = jax.random.split(row_key)
        frequency = jnp.exp(jax.random.uniform(freq_key, (), jnp.float32, math.log(0.02), math.log(0.5)))
        noise = jax.random.normal(noise_key, (DONORS,), jnp.float32)
        logit = jnp.log(frequency / (1.0 - frequency)) + 1.5 * noise
        return 2.0 * jax.nn.sigmoid(logit)
    return jax.vmap(single_row)(variant_ids)


def cis_draw(key):
    tile_key = jax.random.fold_in(key, 5)
    gene = jnp.arange(GENES)
    block = gene // G_DEV
    lowest = jnp.maximum(block * VT_DEV - RIM, 0)
    highest = jnp.minimum((block + 1) * VT_DEV + RIM, VTILES) - K
    offset = jax.random.randint(tile_key, (GENES,), 0, highest - lowest + 1)
    start = lowest + offset
    within = gene % G_DEV
    start = jnp.where(within == 0, lowest, jnp.where(within == 1, highest, start))
    return (start[:, None] + jnp.arange(K)[None, :]).astype(jnp.int32)


def draw_dosage(key, part):
    return dose_rows(key, jnp.arange(VARIANTS)).astype(jnp.bfloat16)


def draw_cis_tiles(key, part):
    return cis_draw(key)


def draw_expression(key, part):
    tiles = cis_draw(key)
    gene = jnp.arange(GENES)
    column = tiles[gene, gene % K]
    variant = column * TILE + gene * 37 % TILE
    planted = dose_rows(key, variant)
    expr_key = jax.random.fold_in(key, 23)
    noise_key, scale_key = jax.random.split(expr_key)
    donor_pos = jnp.arange(DONORS).astype(jnp.float32) / DONORS
    noise = jax.random.normal(noise_key, (GENES, DONORS), jnp.float32)
    factor = 0.5 + donor_pos
    scale = jnp.exp(jax.random.uniform(scale_key, (GENES, 1), jnp.float32, 0.0, math.log(10.0)))
    drawn = noise * scale * factor[None, :]
    strong = 4.0 * (planted - 1.0) + 0.3 * noise
    chosen = gene % 8 == 3
    values = jnp.where(chosen[:, None], strong, drawn)
    return jnp.clip(values, -60.0, 60.0).astype(jnp.bfloat16)


def setup_inputs(seed: int = 0, part: int = 0) -> dict:
    streams_of = jax.random.split(jax.random.key(seed), 4)
    part_keys = jax.random.split(jax.random.fold_in(streams_of[3], part), 4)
    dosage = draw_dosage(jax.random.fold_in(jax.random.fold_in(streams_of[3], part), 71), part)
    expression = draw_expression(jax.random.fold_in(jax.random.fold_in(streams_of[3], part), 71), part)
    cis_tiles = draw_cis_tiles(jax.random.fold_in(jax.random.fold_in(streams_of[3], part), 71), part)
    return dict(dosage=dosage, expression=expression, cis_tiles=cis_tiles)


def beta_log_constant(shape_a):
    inverse = 1.0 / shape_a
    ratio = 0.5 * math.log(shape_a) - inverse / 8.0 + inverse ** 3 / 192.0 + inverse ** 5 / 640.0 - 17.0 * inverse ** 7 / 14336.0
    return ratio - 0.5 * math.log(math.pi)

def standardize(values, count):
    wide = values.astype(jnp.float32)
    totals = lax.optimization_barrier(jnp.sum(wide, axis=1))
    squares = lax.optimization_barrier(jnp.sum(wide * wide, axis=1))
    center = totals / count
    spread = squares / count - center * center
    return ((wide - center[:, None]) * lax.rsqrt(spread + 1e-05)[:, None]).astype(jnp.bfloat16)

def tail_probability(squared, shape_a, log_const, terms):
    narrow = squared < 1.5 / (shape_a + 2.5)
    first = jnp.where(narrow, 0.5, shape_a)
    second = jnp.where(narrow, shape_a, 0.5)
    argument = jnp.where(narrow, squared, 1.0 - squared)
    total_ab = first + second

    def odd_term(index):
        return -(first + index) * (total_ab + index) * argument / ((first + 2.0 * index) * (first + 2.0 * index + 1.0))

    def even_term(index):
        return index * (second - index) * argument / ((first + 2.0 * index - 1.0) * (first + 2.0 * index))

    def advance(carried, coefficient):
        upper_ratio, lower_ratio, estimate = carried
        lower_ratio = 1.0 / (1.0 + coefficient * lower_ratio)
        upper_ratio = 1.0 + coefficient / upper_ratio
        return (upper_ratio, lower_ratio, estimate * lower_ratio * upper_ratio)

    def sweep(turn, carried):
        for offset in range(4):
            index = (4 * turn + offset + 1).astype(jnp.float32)
            carried = advance(carried, even_term(index))
            carried = advance(carried, odd_term(index))
        return carried
    leading = 1.0 / (1.0 - total_ab * argument / (first + 1.0))
    start = (jnp.ones_like(squared), leading, leading)
    carried = lax.fori_loop(0, terms // 4, sweep, start)
    estimate = carried[2]
    front = jnp.sqrt(squared) * jnp.exp(shape_a * jnp.log1p(-squared) + log_const)
    share = front * estimate / first
    return jnp.where(narrow, 1.0 - share, share)

def reference(dosage, expression, cis_tiles):
    zdose = standardize(dosage, DONORS).reshape(VTILES, TILE, DONORS)
    zexpr = standardize(expression, DONORS)

    def block_dots(operands):
        gene_rows, tile_rows = operands
        picked = zdose[tile_rows]
        dots = jnp.einsum('gd,gktd->gkt', gene_rows.astype(jnp.float32), picked.astype(jnp.float32))
        return dots.reshape(gene_rows.shape[0], K * TILE)
    dots = lax.map(block_dots, (zexpr.reshape(GENES // 4, 4, DONORS), cis_tiles.reshape(GENES // 4, 4, K)))
    correlation = dots.reshape(GENES, K * TILE) / DONORS
    squared = jnp.minimum(correlation * correlation, 0.9)
    shape_a = (DONORS - 2) / 2.0
    log_const = beta_log_constant(shape_a)
    pvalue = tail_probability(squared, shape_a, log_const, CF_TERMS)
    return (correlation, pvalue)
```

```python
import functools
import math

import jax
import jax.numpy as jnp
from jax import lax
from jax.experimental import pallas as pl
from jax.experimental.pallas import tpu as pltpu
from jax.sharding import PartitionSpec as P

TILE = 128
CF_TERMS = 32
CHUNKS = 4
ROWS = 256
MESH = pl.DeviceIdType.MESH


def beta_log_constant(shape_a):
    inverse = 1.0 / shape_a
    ratio = (
        0.5 * math.log(shape_a)
        - inverse / 8.0
        + inverse**3 / 192.0
        + inverse**5 / 640.0
        - 17.0 * inverse**7 / 14336.0
    )
    return ratio - 0.5 * math.log(math.pi)


def coefficients(a, b, terms):
    out = [-(a + b) / (a + 1.0)]
    for m in range(1, terms + 1):
        out.append(m * (b - m) / ((a + 2.0 * m - 1.0) * (a + 2.0 * m)))
        out.append(-(a + m) * (a + b + m) / ((a + 2.0 * m) * (a + 2.0 * m + 1.0)))
    return out


def tail_probability(squared, shape_a, log_const, terms):
    narrow = squared < 1.5 / (shape_a + 2.5)
    argument = jnp.where(narrow, squared, 1.0 - squared)
    small = coefficients(0.5, shape_a, terms)
    large = coefficients(shape_a, 0.5, terms)
    level = jnp.ones_like(squared)
    for c_small, c_large in zip(small[::-1], large[::-1]):
        level = 1.0 + jnp.where(narrow, c_small, c_large) * argument / level
    front = jnp.sqrt(squared) * jnp.exp(shape_a * jnp.log1p(-squared) + log_const)
    share = front / (level * jnp.where(narrow, 0.5, shape_a))
    return jnp.where(narrow, 1.0 - share, share)


def lane_sums(block_of, columns, rows):
    total = jnp.zeros((rows, 128), jnp.float32)
    square = jnp.zeros((rows, 128), jnp.float32)
    for j in range(columns // 128):
        x = block_of(j).astype(jnp.float32)
        total = total + x
        square = square + x * x
    return total, square


def dot_t(left, right):
    return lax.dot_general(
        left, right, (((1,), (1,)), ((), ())), preferred_element_type=jnp.float32
    )


def kernel(
    sizes,
    dose_hbm, expr_ref, cis_ref,
    corr_ref, pval_ref,
    dose, zown, zin, cin, mom, mom_in, acc, dstat, dstat_in, prod,
    sel_own, own_in, sel_nbr, nbr_in, ret, ret_in,
    dose_sem, z_send, z_recv, c_send, c_recv, s_send, s_recv, r_send, r_recv,
):
    genes, local, variants, regions, donors = sizes
    tiles = variants // TILE
    width = local // CHUNKS
    half = corr_ref.shape[1]
    half_k = half // TILE
    me = lax.axis_index("region")
    core = lax.axis_index("donor")
    has_prev = me > 0
    has_next = me < regions - 1
    prev = jnp.maximum(me - 1, 0)
    nxt = jnp.minimum(me + 1, regions - 1)
    sibling = {"donor": 1 - core}
    sides = ((0, has_prev, {"region": prev}), (1, has_next, {"region": nxt}))

    barrier = pltpu.get_barrier_semaphore()
    pl.semaphore_signal(barrier, inc=1, device_id=sibling, device_id_type=MESH)
    for _, there, where in sides:
        @pl.when(there)
        def _():
            pl.semaphore_signal(barrier, inc=1, device_id=where, device_id_type=MESH)

    blocks = variants // ROWS
    loads = [
        pltpu.make_async_copy(
            dose_hbm.at[pl.ds(i * ROWS, ROWS)], dose.at[pl.ds(i * ROWS, ROWS)], dose_sem.at[i]
        )
        for i in range(blocks)
    ]
    for load in loads:
        load.start()

    total, square = lane_sums(lambda j: expr_ref[:, j * 128:(j + 1) * 128], local, genes)
    total = jnp.sum(total, axis=1, keepdims=True)
    square = jnp.sum(square, axis=1, keepdims=True)
    lane = lax.broadcasted_iota(jnp.int32, (genes, 128), 1)
    mom[...] = jnp.where(lane == 0, total, square)
    for side in range(2):
        @pl.when(jnp.logical_not(sides[side][1]))
        def _():
            zin[:, pl.ds(side * genes, genes), :] = jnp.zeros((CHUNKS, genes, width), jnp.bfloat16)
            cin[side] = jnp.zeros(cis_ref.shape, jnp.int32)

    pl.semaphore_wait(barrier, 1 + has_prev.astype(jnp.int32) + has_next.astype(jnp.int32))

    def to_sibling(src, dst, slot):
        return pltpu.make_async_remote_copy(
            src_ref=src, dst_ref=dst, send_sem=s_send.at[slot], recv_sem=s_recv.at[slot],
            device_id=sibling, device_id_type=MESH,
        )

    mom_copy = to_sibling(mom, mom_in, 0)
    mom_copy.start()

    def cis_copy(side):
        return pltpu.make_async_remote_copy(
            src_ref=cis_ref, dst_ref=cin.at[1 - side], send_sem=c_send.at[side],
            recv_sem=c_recv.at[1 - side], device_id=sides[side][2], device_id_type=MESH,
        )

    def z_copy(side, j):
        return pltpu.make_async_remote_copy(
            src_ref=zown.at[j], dst_ref=zin.at[j, pl.ds((1 - side) * genes, genes)],
            send_sem=z_send.at[side, j], recv_sem=z_recv.at[1 - side, j],
            device_id=sides[side][2], device_id_type=MESH,
        )

    def z_arrival(side, j):
        return pltpu.make_async_remote_copy(
            src_ref=zown.at[j], dst_ref=zin.at[j, pl.ds(side * genes, genes)],
            send_sem=z_send.at[side, j], recv_sem=z_recv.at[side, j],
            device_id=sides[side][2], device_id_type=MESH,
        )

    def cis_arrival(side):
        return pltpu.make_async_remote_copy(
            src_ref=cis_ref, dst_ref=cin.at[side], send_sem=c_send.at[side],
            recv_sem=c_recv.at[side], device_id=sides[side][2], device_id_type=MESH,
        )

    def ret_copy(side):
        return pltpu.make_async_remote_copy(
            src_ref=ret.at[pl.ds(side * genes, genes)], dst_ref=ret_in.at[1 - side],
            send_sem=r_send.at[side], recv_sem=r_recv.at[1 - side],
            device_id=sides[side][2], device_id_type=MESH,
        )

    def ret_arrival(side):
        return pltpu.make_async_remote_copy(
            src_ref=ret.at[pl.ds(side * genes, genes)], dst_ref=ret_in.at[side],
            send_sem=r_send.at[side], recv_sem=r_recv.at[side],
            device_id=sides[side][2], device_id_type=MESH,
        )

    mom_copy.wait_recv()
    sums = mom[...] + mom_in[...]
    center = sums[:, 0:1] / donors
    spread = sums[:, 1:2] / donors - center * center
    scale = lax.rsqrt(spread + 1e-05)
    z_sum = jnp.zeros((genes, 1), jnp.float32)
    for j in range(CHUNKS):
        y = expr_ref[:, j * width:(j + 1) * width].astype(jnp.float32)
        z = ((y - center) * scale).astype(jnp.bfloat16)
        zown[j] = z
        for side, there, _ in sides:
            @pl.when(there)
            def _():
                z_copy(side, j).start()
        z_sum = z_sum + jnp.sum(z.astype(jnp.float32), axis=1, keepdims=True)
    for side, there, _ in sides:
        @pl.when(there)
        def _():
            cis_copy(side).start()

    group = 32
    for i in range(blocks):
        loads[i].wait()

        def row_group(q, carry):
            start = pl.multiple_of(i * ROWS + q * group, group)
            rows = pl.ds(start, group)
            t, s = lane_sums(lambda j: dose[rows, j * 128:(j + 1) * 128], local, group)
            acc[0, rows] = t
            acc[1, rows] = s
            return carry

        lax.fori_loop(0, ROWS // group, row_group, 0)
        for w in range(2):
            for h in range(ROWS // 128):
                at = i * ROWS + h * 128
                turned = jnp.transpose(acc[w, at:at + 128])
                dstat[w:w + 1, at:at + 128] = jnp.sum(turned, axis=0, keepdims=True)
    stat_copy = to_sibling(dstat, dstat_in, 1)
    stat_copy.start()

    def own_block(i, carry):
        rows = pl.ds(pl.multiple_of(i * ROWS, ROWS), ROWS)
        part = dot_t(zown[0], dose[rows, 0:width])
        for j in range(1, CHUNKS):
            part = part + dot_t(zown[j], dose[rows, j * width:(j + 1) * width])
        prod[0:genes, rows] = part
        return carry

    lax.fori_loop(0, blocks, own_block, 0)

    stat_copy.wait_recv()
    mean = (dstat[0:1, :] + dstat_in[0:1, :]) / donors
    var = (dstat[1:2, :] + dstat_in[1:2, :]) / donors - mean * mean
    rstd = lax.rsqrt(var + 1e-05)

    base = me * tiles

    def select(first, cis, sums_z, put):
        for t in range(tiles):
            cols = slice(t * TILE, (t + 1) * TILE)
            prod[first:first + genes, cols] = (
                prod[first:first + genes, cols] - mean[:, cols] * sums_z
            ) * rstd[:, cols]
        for k in range(2 * half_k):
            here = cis[:, k:k + 1] - base
            picked = jnp.zeros((genes, TILE), jnp.float32)
            for t in range(tiles):
                picked = jnp.where(
                    here == t, prod[first:first + genes, t * TILE:(t + 1) * TILE], picked
                )
            put(k // half_k, (k % half_k) * TILE, picked)

    def put_own(h, at, value):
        sel_own[h, :, at:at + TILE] = value

    select(0, cis_ref[...], z_sum, put_own)
    own_copy = to_sibling(sel_own.at[1 - core], own_in, 2)
    own_copy.start()

    z_sums = jnp.zeros((2 * genes, 1), jnp.float32)
    for j in range(CHUNKS):
        for side, there, _ in sides:
            @pl.when(there)
            def _():
                z_arrival(side, j).wait_recv()
        z_sums = z_sums + jnp.sum(zin[j].astype(jnp.float32), axis=1, keepdims=True)

        def nbr_block(i, carry):
            rows = pl.ds(pl.multiple_of(i * ROWS, ROWS), ROWS)
            part = dot_t(zin[j], dose[rows, j * width:(j + 1) * width])
            if j:
                part = part + prod[genes:3 * genes, rows]
            prod[genes:3 * genes, rows] = part
            return carry

        lax.fori_loop(0, blocks, nbr_block, 0)

    for side, there, _ in sides:
        @pl.when(there)
        def _():
            cis_arrival(side).wait_recv()

        def put_nbr(h, at, value):
            sel_nbr[h, side * genes:(side + 1) * genes, at:at + TILE] = value

        select((side + 1) * genes, cin[side], z_sums[side * genes:(side + 1) * genes], put_nbr)
    nbr_copy = to_sibling(sel_nbr.at[1 - core], nbr_in, 3)
    nbr_copy.start()
    nbr_copy.wait_recv()
    ret[...] = sel_nbr[core] + nbr_in[...]
    for side, there, _ in sides:
        @pl.when(there)
        def _():
            ret_copy(side).start()

    own_copy.wait_recv()
    corr_ref[...] = sel_own[core] + own_in[...]
    for side, there, _ in sides:
        @pl.when(there)
        def _():
            ret_arrival(side).wait_recv()
            corr_ref[...] += ret_in[side]
    correlation = corr_ref[...] / donors
    corr_ref[...] = correlation
    squared = jnp.minimum(correlation * correlation, 0.9)
    shape_a = (donors - 2) / 2.0
    pval_ref[...] = tail_probability(squared, shape_a, beta_log_constant(shape_a), CF_TERMS)

    for copy in (mom_copy, stat_copy, own_copy, nbr_copy):
        copy.wait_send()
    for side, there, _ in sides:
        @pl.when(there)
        def _():
            cis_copy(side).wait_send()
            ret_copy(side).wait_send()
            for j in range(CHUNKS):
                z_copy(side, j).wait_send()


def shards(dosage, expression, cis_tiles):
    variants, local = dosage.shape
    genes = expression.shape[0]
    cores = lax.axis_size("donor")
    regions = lax.axis_size("region")
    window = cis_tiles.shape[1]
    half = window * TILE // cores
    width = local // CHUNKS
    sizes = (genes, local, variants, regions, local * cores)
    f32, bf16 = jnp.float32, jnp.bfloat16
    dma = pltpu.SemaphoreType.DMA
    vmem = pl.BlockSpec(memory_space=pltpu.VMEM)
    return pl.pallas_call(
        functools.partial(kernel, sizes),
        out_shape=(
            jax.ShapeDtypeStruct((genes, half), f32),
            jax.ShapeDtypeStruct((genes, half), f32),
        ),
        in_specs=[pl.BlockSpec(memory_space=pl.ANY), vmem, vmem],
        out_specs=(vmem, vmem),
        scratch_shapes=[
            pltpu.VMEM((variants, local), bf16),
            pltpu.VMEM((CHUNKS, genes, width), bf16),
            pltpu.VMEM((CHUNKS, 2 * genes, width), bf16),
            pltpu.VMEM((2, genes, window), jnp.int32),
            pltpu.VMEM((genes, 128), f32),
            pltpu.VMEM((genes, 128), f32),
            pltpu.VMEM((2, variants, 128), f32),
            pltpu.VMEM((2, variants), f32),
            pltpu.VMEM((2, variants), f32),
            pltpu.VMEM((3 * genes, variants), f32),
            pltpu.VMEM((2, genes, half), f32),
            pltpu.VMEM((genes, half), f32),
            pltpu.VMEM((2, 2 * genes, half), f32),
            pltpu.VMEM((2 * genes, half), f32),
            pltpu.VMEM((2 * genes, half), f32),
            pltpu.VMEM((2, genes, half), f32),
            dma((variants // ROWS,)),
            dma((2, CHUNKS)),
            dma((2, CHUNKS)),
            dma((2,)),
            dma((2,)),
            dma((4,)),
            dma((4,)),
            dma((2,)),
            dma((2,)),
        ],
        compiler_params=pltpu.CompilerParams(
            collective_id=0, has_side_effects=True, vmem_limit_bytes=40 * 1024 * 1024
        ),
    )(dosage, expression, cis_tiles)


def solution(mesh):
    assert mesh.shape["donor"] == 2
    in_specs = (
        P(("grp", "region"), "donor"),
        P(("grp", "region"), "donor"),
        P(("grp", "region"), None),
    )
    out_specs = (P(("grp", "region"), "donor"), P(("grp", "region"), "donor"))
    return jax.shard_map(shards, mesh=mesh, in_specs=in_specs, out_specs=out_specs, check_vma=False)
```

```python
import functools
import math

import jax
import jax.numpy as jnp
from jax import lax
from jax.experimental import pallas as pl
from jax.experimental.pallas import tpu as pltpu
from jax.sharding import PartitionSpec as P

TILE = 128
CF_TERMS = 32
CHUNKS = 4
ROWS = 256
MESH = pl.DeviceIdType.MESH


def beta_log_constant(shape_a):
    inverse = 1.0 / shape_a
    ratio = (
        0.5 * math.log(shape_a)
        - inverse / 8.0
        + inverse**3 / 192.0
        + inverse**5 / 640.0
        - 17.0 * inverse**7 / 14336.0
    )
    return ratio - 0.5 * math.log(math.pi)


def coefficients(a, b, terms):
    out = [-(a + b) / (a + 1.0)]
    for m in range(1, terms + 1):
        out.append(m * (b - m) / ((a + 2.0 * m - 1.0) * (a + 2.0 * m)))
        out.append(-(a + m) * (a + b + m) / ((a + 2.0 * m) * (a + 2.0 * m + 1.0)))
    return out


def tail_probability(squared, shape_a, log_const, terms):
    narrow = squared < 1.5 / (shape_a + 2.5)
    argument = jnp.where(narrow, squared, 1.0 - squared)
    small = coefficients(0.5, shape_a, terms)
    large = coefficients(shape_a, 0.5, terms)
    level = jnp.ones_like(squared)
    for c_small, c_large in zip(small[::-1], large[::-1]):
        level = 1.0 + jnp.where(narrow, c_small, c_large) * argument / level
    front = jnp.sqrt(squared) * jnp.exp(shape_a * jnp.log1p(-squared) + log_const)
    share = front / (level * jnp.where(narrow, 0.5, shape_a))
    return jnp.where(narrow, 1.0 - share, share)


def lane_sums(block_of, columns, rows):
    total = jnp.zeros((rows, 128), jnp.float32)
    square = jnp.zeros((rows, 128), jnp.float32)
    for j in range(columns // 128):
        x = block_of(j).astype(jnp.float32)
        total = total + x
        square = square + x * x
    return total, square


def dot_t(left, right):
    return lax.dot_general(
        left, right, (((1,), (1,)), ((), ())), preferred_element_type=jnp.float32
    )


def kernel(
    sizes,
    dose_hbm, expr_hbm, cis_t,
    corr_ref, pval_ref,
    dose, expr_ref, cis_ref, zown, zin, cin, mom, mom_in, mom_all, nbr_mom, acc, dstat, dstat_in, prod,
    sel_own, own_in, sel_nbr, nbr_in, ret, ret_in,
    dose_sem, expr_sem, z_send, z_recv, c_send, c_recv, m_send, m_recv, s_send, s_recv, r_send, r_recv,
):
    genes, local, variants, regions, donors = sizes
    tiles = variants // TILE
    width = local // CHUNKS
    half = corr_ref.shape[1]
    half_k = half // TILE
    me = lax.axis_index("region")
    core = lax.axis_index("donor")
    has_prev = me > 0
    has_next = me < regions - 1
    prev = jnp.maximum(me - 1, 0)
    nxt = jnp.minimum(me + 1, regions - 1)
    sibling = {"donor": 1 - core}
    sides = ((0, has_prev, {"region": prev}), (1, has_next, {"region": nxt}))

    barrier = pltpu.get_barrier_semaphore()
    pl.semaphore_signal(barrier, inc=1, device_id=sibling, device_id_type=MESH)
    for _, there, where in sides:
        @pl.when(there)
        def _():
            pl.semaphore_signal(barrier, inc=1, device_id=where, device_id_type=MESH)

    expr_load = pltpu.make_async_copy(expr_hbm, expr_ref, expr_sem)
    expr_load.start()
    blocks = variants // ROWS
    loads = [
        pltpu.make_async_copy(
            dose_hbm.at[pl.ds(i * ROWS, ROWS)], dose.at[pl.ds(i * ROWS, ROWS)], dose_sem.at[i]
        )
        for i in range(blocks)
    ]
    for load in loads:
        load.start()

    cis_ref[...] = jnp.transpose(cis_t[...])
    expr_load.wait()
    total, square = lane_sums(lambda j: expr_ref[:, j * 128:(j + 1) * 128], local, genes)
    total = jnp.sum(total, axis=1, keepdims=True)
    square = jnp.sum(square, axis=1, keepdims=True)
    lane = lax.broadcasted_iota(jnp.int32, (genes, 128), 1)
    mom[...] = jnp.where(lane == 0, total, square)
    for side in range(2):
        @pl.when(jnp.logical_not(sides[side][1]))
        def _():
            zin[:, pl.ds(side * genes, genes), :] = jnp.zeros((CHUNKS, genes, width), jnp.bfloat16)
            cin[side] = jnp.zeros(cis_ref.shape, jnp.int32)
            nbr_mom[side] = jnp.zeros((genes, 128), jnp.float32)

    pl.semaphore_wait(barrier, 1 + has_prev.astype(jnp.int32) + has_next.astype(jnp.int32))

    def to_sibling(src, dst, slot):
        return pltpu.make_async_remote_copy(
            src_ref=src, dst_ref=dst, send_sem=s_send.at[slot], recv_sem=s_recv.at[slot],
            device_id=sibling, device_id_type=MESH,
        )

    def cis_copy(side):
        return pltpu.make_async_remote_copy(
            src_ref=cis_ref, dst_ref=cin.at[1 - side], send_sem=c_send.at[side],
            recv_sem=c_recv.at[1 - side], device_id=sides[side][2], device_id_type=MESH,
        )

    def z_copy(side, j):
        return pltpu.make_async_remote_copy(
            src_ref=expr_hbm.at[:, pl.ds(j * width, width)], dst_ref=zin.at[j, pl.ds((1 - side) * genes, genes)],
            send_sem=z_send.at[side, j], recv_sem=z_recv.at[1 - side, j],
            device_id=sides[side][2], device_id_type=MESH,
        )

    def z_arrival(side, j):
        return pltpu.make_async_remote_copy(
            src_ref=expr_hbm.at[:, pl.ds(j * width, width)], dst_ref=zin.at[j, pl.ds(side * genes, genes)],
            send_sem=z_send.at[side, j], recv_sem=z_recv.at[side, j],
            device_id=sides[side][2], device_id_type=MESH,
        )

    def cis_arrival(side):
        return pltpu.make_async_remote_copy(
            src_ref=cis_ref, dst_ref=cin.at[side], send_sem=c_send.at[side],
            recv_sem=c_recv.at[side], device_id=sides[side][2], device_id_type=MESH,
        )

    def mom_out(side):
        return pltpu.make_async_remote_copy(
            src_ref=mom_all, dst_ref=nbr_mom.at[1 - side], send_sem=m_send.at[side],
            recv_sem=m_recv.at[1 - side], device_id=sides[side][2], device_id_type=MESH,
        )

    def mom_arrival(side):
        return pltpu.make_async_remote_copy(
            src_ref=mom_all, dst_ref=nbr_mom.at[side], send_sem=m_send.at[side],
            recv_sem=m_recv.at[side], device_id=sides[side][2], device_id_type=MESH,
        )

    def ret_copy(side):
        return pltpu.make_async_remote_copy(
            src_ref=ret.at[pl.ds(side * genes, genes)], dst_ref=ret_in.at[1 - side],
            send_sem=r_send.at[side], recv_sem=r_recv.at[1 - side],
            device_id=sides[side][2], device_id_type=MESH,
        )

    def ret_arrival(side):
        return pltpu.make_async_remote_copy(
            src_ref=ret.at[pl.ds(side * genes, genes)], dst_ref=ret_in.at[side],
            send_sem=r_send.at[side], recv_sem=r_recv.at[side],
            device_id=sides[side][2], device_id_type=MESH,
        )

    mom_copy = to_sibling(mom, mom_in, 0)
    mom_copy.start()
    for side, there, _ in sides:
        @pl.when(there)
        def _():
            cis_copy(side).start()
            for j in range(CHUNKS):
                z_copy(side, j).start()

    def standard(y, sums):
        center = sums[:, 0:1] / donors
        spread = sums[:, 1:2] / donors - center * center
        scale = lax.rsqrt(spread + 1e-05)
        return ((y.astype(jnp.float32) - center) * scale).astype(jnp.bfloat16)

    group = 32
    z_sum = jnp.zeros((genes, 1), jnp.float32)
    for i in range(blocks):
        loads[i].wait()

        def row_group(q, carry):
            start = pl.multiple_of(i * ROWS + q * group, group)
            rows = pl.ds(start, group)
            t, s = lane_sums(lambda j: dose[rows, j * 128:(j + 1) * 128], local, group)
            acc[0, rows] = t
            acc[1, rows] = s
            return carry

        lax.fori_loop(0, ROWS // group, row_group, 0)
        for w in range(2):
            for h in range(ROWS // 128):
                at = i * ROWS + h * 128
                turned = jnp.transpose(acc[w, at:at + 128])
                dstat[w:w + 1, at:at + 128] = jnp.sum(turned, axis=0, keepdims=True)
        if i == blocks // 2 - 1:
            mom_copy.wait_recv()
            mom_all[...] = mom[...] + mom_in[...]
            for side, there, _ in sides:
                @pl.when(there)
                def _():
                    mom_out(side).start()
            for j in range(CHUNKS):
                z = standard(expr_ref[:, j * width:(j + 1) * width], mom_all[...])
                zown[j] = z
                z_sum = z_sum + jnp.sum(z.astype(jnp.float32), axis=1, keepdims=True)
    stat_copy = to_sibling(dstat, dstat_in, 1)
    stat_copy.start()

    def own_block(i, carry):
        rows = pl.ds(pl.multiple_of(i * ROWS, ROWS), ROWS)
        part = dot_t(zown[0], dose[rows, 0:width])
        for j in range(1, CHUNKS):
            part = part + dot_t(zown[j], dose[rows, j * width:(j + 1) * width])
        prod[0:genes, rows] = part
        return carry

    lax.fori_loop(0, blocks, own_block, 0)

    stat_copy.wait_recv()
    mean = (dstat[0:1, :] + dstat_in[0:1, :]) / donors
    var = (dstat[1:2, :] + dstat_in[1:2, :]) / donors - mean * mean
    rstd = lax.rsqrt(var + 1e-05)

    base = me * tiles

    def select(first, cis, sums_z, put):
        for t in range(tiles):
            cols = slice(t * TILE, (t + 1) * TILE)
            prod[first:first + genes, cols] = (
                prod[first:first + genes, cols] - mean[:, cols] * sums_z
            ) * rstd[:, cols]
        for k in range(2 * half_k):
            here = cis[:, k:k + 1] - base
            picked = jnp.zeros((genes, TILE), jnp.float32)
            for t in range(tiles):
                picked = jnp.where(
                    here == t, prod[first:first + genes, t * TILE:(t + 1) * TILE], picked
                )
            put(k // half_k, (k % half_k) * TILE, picked)

    def put_own(h, at, value):
        sel_own[h, :, at:at + TILE] = value

    select(0, cis_ref[...], z_sum, put_own)
    own_copy = to_sibling(sel_own.at[1 - core], own_in, 2)
    own_copy.start()

    z_sums = jnp.zeros((2 * genes, 1), jnp.float32)
    for side, there, _ in sides:
        @pl.when(there)
        def _():
            cis_arrival(side).wait_recv()
            mom_arrival(side).wait_recv()
    nbr_sums = nbr_mom[...].reshape(2 * genes, 128)
    for j in range(CHUNKS):
        for side, there, _ in sides:
            @pl.when(there)
            def _():
                z_arrival(side, j).wait_recv()
        z = standard(zin[j], nbr_sums)
        zin[j] = z
        z_sums = z_sums + jnp.sum(z.astype(jnp.float32), axis=1, keepdims=True)

        def nbr_block(i, carry):
            rows = pl.ds(pl.multiple_of(i * ROWS, ROWS), ROWS)
            part = dot_t(zin[j], dose[rows, j * width:(j + 1) * width])
            if j:
                part = part + prod[genes:3 * genes, rows]
            prod[genes:3 * genes, rows] = part
            return carry

        lax.fori_loop(0, blocks, nbr_block, 0)

    for side in range(2):
        def put_nbr(h, at, value):
            sel_nbr[h, side * genes:(side + 1) * genes, at:at + TILE] = value

        select((side + 1) * genes, cin[side], z_sums[side * genes:(side + 1) * genes], put_nbr)
    nbr_copy = to_sibling(sel_nbr.at[1 - core], nbr_in, 3)
    nbr_copy.start()
    nbr_copy.wait_recv()
    ret[...] = sel_nbr[core] + nbr_in[...]
    for side, there, _ in sides:
        @pl.when(there)
        def _():
            ret_copy(side).start()

    own_copy.wait_recv()
    corr_ref[...] = sel_own[core] + own_in[...]
    for side, there, _ in sides:
        @pl.when(there)
        def _():
            ret_arrival(side).wait_recv()
            corr_ref[...] += ret_in[side]
    correlation = corr_ref[...] / donors
    corr_ref[...] = correlation
    squared = jnp.minimum(correlation * correlation, 0.9)
    shape_a = (donors - 2) / 2.0
    pval_ref[...] = tail_probability(squared, shape_a, beta_log_constant(shape_a), CF_TERMS)

    for copy in (mom_copy, stat_copy, own_copy, nbr_copy):
        copy.wait_send()
    for side, there, _ in sides:
        @pl.when(there)
        def _():
            cis_copy(side).wait_send()
            mom_out(side).wait_send()
            ret_copy(side).wait_send()
            for j in range(CHUNKS):
                z_copy(side, j).wait_send()


def shards(dosage, expression, cis_tiles):
    variants, local = dosage.shape
    genes = expression.shape[0]
    cores = lax.axis_size("donor")
    regions = lax.axis_size("region")
    window = cis_tiles.shape[1]
    half = window * TILE // cores
    width = local // CHUNKS
    sizes = (genes, local, variants, regions, local * cores)
    f32, bf16 = jnp.float32, jnp.bfloat16
    dma = pltpu.SemaphoreType.DMA
    vmem = pl.BlockSpec(memory_space=pltpu.VMEM)
    hbm = pl.BlockSpec(memory_space=pltpu.HBM)
    return pl.pallas_call(
        functools.partial(kernel, sizes),
        out_shape=(
            jax.ShapeDtypeStruct((genes, half), f32),
            jax.ShapeDtypeStruct((genes, half), f32),
        ),
        in_specs=[hbm, hbm, vmem],
        out_specs=(vmem, vmem),
        scratch_shapes=[
            pltpu.VMEM((variants, local), bf16),
            pltpu.VMEM((genes, local), bf16),
            pltpu.VMEM((genes, window), jnp.int32),
            pltpu.VMEM((CHUNKS, genes, width), bf16),
            pltpu.VMEM((CHUNKS, 2 * genes, width), bf16),
            pltpu.VMEM((2, genes, window), jnp.int32),
            pltpu.VMEM((genes, 128), f32),
            pltpu.VMEM((genes, 128), f32),
            pltpu.VMEM((genes, 128), f32),
            pltpu.VMEM((2, genes, 128), f32),
            pltpu.VMEM((2, variants, 128), f32),
            pltpu.VMEM((2, variants), f32),
            pltpu.VMEM((2, variants), f32),
            pltpu.VMEM((3 * genes, variants), f32),
            pltpu.VMEM((2, genes, half), f32),
            pltpu.VMEM((genes, half), f32),
            pltpu.VMEM((2, 2 * genes, half), f32),
            pltpu.VMEM((2 * genes, half), f32),
            pltpu.VMEM((2 * genes, half), f32),
            pltpu.VMEM((2, genes, half), f32),
            dma((variants // ROWS,)),
            dma,
            dma((2, CHUNKS)),
            dma((2, CHUNKS)),
            dma((2,)),
            dma((2,)),
            dma((2,)),
            dma((2,)),
            dma((4,)),
            dma((4,)),
            dma((2,)),
            dma((2,)),
        ],
        compiler_params=pltpu.CompilerParams(
            collective_id=0, has_side_effects=True, vmem_limit_bytes=40 * 1024 * 1024
        ),
    )(dosage, expression, cis_tiles.T)


def solution(mesh):
    assert mesh.shape["donor"] == 2
    in_specs = (
        P(("grp", "region"), "donor"),
        P(("grp", "region"), "donor"),
        P(("grp", "region"), None),
    )
    out_specs = (P(("grp", "region"), "donor"), P(("grp", "region"), "donor"))
    return jax.shard_map(shards, mesh=mesh, in_specs=in_specs, out_specs=out_specs, check_vma=False)
```

```python
import functools
import math

import jax
import jax.numpy as jnp
from jax import lax
from jax.experimental import pallas as pl
from jax.experimental.pallas import tpu as pltpu
from jax.sharding import PartitionSpec as P

TILE = 128
CF_TERMS = 32
CHUNKS = 4
ROWS = 256
MESH = pl.DeviceIdType.MESH


def beta_log_constant(shape_a):
    inverse = 1.0 / shape_a
    ratio = (
        0.5 * math.log(shape_a)
        - inverse / 8.0
        + inverse**3 / 192.0
        + inverse**5 / 640.0
        - 17.0 * inverse**7 / 14336.0
    )
    return ratio - 0.5 * math.log(math.pi)


def coefficients(a, b, terms):
    out = [-(a + b) / (a + 1.0)]
    for m in range(1, terms + 1):
        out.append(m * (b - m) / ((a + 2.0 * m - 1.0) * (a + 2.0 * m)))
        out.append(-(a + m) * (a + b + m) / ((a + 2.0 * m) * (a + 2.0 * m + 1.0)))
    return out


def tail_probability(squared, shape_a, log_const, terms):
    narrow = squared < 1.5 / (shape_a + 2.5)
    argument = jnp.where(narrow, squared, 1.0 - squared)
    small = coefficients(0.5, shape_a, terms)
    large = coefficients(shape_a, 0.5, terms)
    level = jnp.ones_like(squared)
    for c_small, c_large in zip(small[::-1], large[::-1]):
        level = 1.0 + jnp.where(narrow, c_small, c_large) * argument / level
    front = jnp.sqrt(squared) * jnp.exp(shape_a * jnp.log1p(-squared) + log_const)
    share = front / (level * jnp.where(narrow, 0.5, shape_a))
    return jnp.where(narrow, 1.0 - share, share)


def lane_sums(block_of, columns, rows):
    total = jnp.zeros((rows, 128), jnp.float32)
    square = jnp.zeros((rows, 128), jnp.float32)
    for j in range(columns // 128):
        x = block_of(j).astype(jnp.float32)
        total = total + x
        square = square + x * x
    return total, square


def dot_t(left, right):
    return lax.dot_general(
        left, right, (((1,), (1,)), ((), ())), preferred_element_type=jnp.float32
    )


def kernel(
    sizes,
    dose_hbm, expr_hbm, cis_t,
    corr_ref, pval_ref,
    dose, expr_ref, cis_ref, zown, zin, cin, mom, mom_in, acc, dstat, dstat_in, prod,
    sel_own, own_in, sel_nbr, nbr_in, ret, ret_in,
    dose_sem, expr_sem, z_send, f_send, z_recv, c_send, c_recv, s_send, s_recv, r_send, r_recv,
):
    genes, local, variants, regions, donors = sizes
    tiles = variants // TILE
    width = local // CHUNKS
    half = corr_ref.shape[1]
    half_k = half // TILE
    me = lax.axis_index("region")
    core = lax.axis_index("donor")
    has_prev = me > 0
    has_next = me < regions - 1
    prev = jnp.maximum(me - 1, 0)
    nxt = jnp.minimum(me + 1, regions - 1)
    sibling = {"donor": 1 - core}
    sides = ((0, has_prev, {"region": prev}), (1, has_next, {"region": nxt}))

    barrier = pltpu.get_barrier_semaphore()
    pl.semaphore_signal(barrier, inc=1, device_id=sibling, device_id_type=MESH)
    for _, there, where in sides:
        @pl.when(there)
        def _():
            pl.semaphore_signal(barrier, inc=1, device_id=where, device_id_type=MESH)

    odd = lax.rem(me, 2)
    far_slot, near_slot = odd, 1 - odd
    partner, ahead, behind = me + 1 - 2 * odd, me + 2 - 4 * odd, me - 2 + 4 * odd
    has_ahead = jnp.logical_and(ahead >= 0, ahead < regions)
    has_far = jnp.logical_and(behind >= 0, behind < regions)
    ahead = jnp.clip(ahead, 0, regions - 1)
    behind = jnp.clip(behind, 0, regions - 1)
    for there, where in ((has_ahead, ahead), (has_far, behind)):
        @pl.when(there)
        def _():
            pl.semaphore_signal(
                barrier, inc=1, device_id={"region": where}, device_id_type=MESH
            )

    expr_load = pltpu.make_async_copy(expr_hbm, expr_ref, expr_sem)
    expr_load.start()
    blocks = variants // ROWS
    loads = [
        pltpu.make_async_copy(
            dose_hbm.at[pl.ds(i * ROWS, ROWS)], dose.at[pl.ds(i * ROWS, ROWS)], dose_sem.at[i]
        )
        for i in range(blocks)
    ]
    for load in loads:
        load.start()

    cis_ref[...] = jnp.transpose(cis_t[...])
    expr_load.wait()
    total, square = lane_sums(lambda j: expr_ref[:, j * 128:(j + 1) * 128], local, genes)
    total = jnp.sum(total, axis=1, keepdims=True)
    square = jnp.sum(square, axis=1, keepdims=True)
    lane = lax.broadcasted_iota(jnp.int32, (genes, 128), 1)
    mom[...] = jnp.where(lane == 0, total, square)
    @pl.when(jnp.logical_not(has_far))
    def _():
        zin[:, far_slot] = jnp.zeros((CHUNKS, genes, width), jnp.bfloat16)
        cin[far_slot] = jnp.zeros(cis_ref.shape, jnp.int32)

    greeted = 1
    for there in (has_prev, has_next, has_ahead, has_far):
        greeted = greeted + there.astype(jnp.int32)
    pl.semaphore_wait(barrier, greeted)

    def to_sibling(src, dst, slot):
        return pltpu.make_async_remote_copy(
            src_ref=src, dst_ref=dst, send_sem=s_send.at[slot], recv_sem=s_recv.at[slot],
            device_id=sibling, device_id_type=MESH,
        )

    mom_copy = to_sibling(mom, mom_in, 0)
    mom_copy.start()

    def cis_copy(side):
        return pltpu.make_async_remote_copy(
            src_ref=cis_ref, dst_ref=cin.at[1 - side], send_sem=c_send.at[side],
            recv_sem=c_recv.at[1 - side], device_id=sides[side][2], device_id_type=MESH,
        )

    def z_copy(j):
        return pltpu.make_async_remote_copy(
            src_ref=zown.at[j], dst_ref=zin.at[j, far_slot], send_sem=z_send.at[j],
            recv_sem=z_recv.at[far_slot, j], device_id={"region": partner}, device_id_type=MESH,
        )

    def z_onward(j):
        return pltpu.make_async_remote_copy(
            src_ref=zin.at[j, near_slot], dst_ref=zin.at[j, far_slot], send_sem=f_send.at[j],
            recv_sem=z_recv.at[far_slot, j], device_id={"region": ahead}, device_id_type=MESH,
        )

    def z_near(j):
        return pltpu.make_async_remote_copy(
            src_ref=zown.at[j], dst_ref=zin.at[j, near_slot], send_sem=z_send.at[j],
            recv_sem=z_recv.at[near_slot, j], device_id={"region": partner}, device_id_type=MESH,
        )

    def pass_on(chunks):
        for j in chunks:
            z_near(j).wait_recv()

            @pl.when(has_ahead)
            def _():
                z_onward(j).start()

    def cis_arrival(side):
        return pltpu.make_async_remote_copy(
            src_ref=cis_ref, dst_ref=cin.at[side], send_sem=c_send.at[side],
            recv_sem=c_recv.at[side], device_id=sides[side][2], device_id_type=MESH,
        )

    def ret_copy(side):
        return pltpu.make_async_remote_copy(
            src_ref=ret.at[pl.ds(side * genes, genes)], dst_ref=ret_in.at[1 - side],
            send_sem=r_send.at[side], recv_sem=r_recv.at[1 - side],
            device_id=sides[side][2], device_id_type=MESH,
        )

    def ret_arrival(side):
        return pltpu.make_async_remote_copy(
            src_ref=ret.at[pl.ds(side * genes, genes)], dst_ref=ret_in.at[side],
            send_sem=r_send.at[side], recv_sem=r_recv.at[side],
            device_id=sides[side][2], device_id_type=MESH,
        )

    for side, there, _ in sides:
        @pl.when(there)
        def _():
            cis_copy(side).start()

    group = 32
    z_sum = jnp.zeros((genes, 1), jnp.float32)
    for i in range(blocks):
        loads[i].wait()

        def row_group(q, carry):
            start = pl.multiple_of(i * ROWS + q * group, group)
            rows = pl.ds(start, group)
            t, s = lane_sums(lambda j: dose[rows, j * 128:(j + 1) * 128], local, group)
            acc[0, rows] = t
            acc[1, rows] = s
            return carry

        lax.fori_loop(0, ROWS // group, row_group, 0)
        if i == 0:
            mom_copy.wait_recv()
            sums = mom[...] + mom_in[...]
            center = sums[:, 0:1] / donors
            spread = sums[:, 1:2] / donors - center * center
            scale = lax.rsqrt(spread + 1e-05)
            for j in range(CHUNKS):
                y = expr_ref[:, j * width:(j + 1) * width].astype(jnp.float32)
                z = ((y - center) * scale).astype(jnp.bfloat16)
                zown[j] = z
                z_copy(j).start()
                z_sum = z_sum + jnp.sum(z.astype(jnp.float32), axis=1, keepdims=True)
        for w in range(2):
            for h in range(ROWS // 128):
                at = i * ROWS + h * 128
                turned = jnp.transpose(acc[w, at:at + 128])
                dstat[w:w + 1, at:at + 128] = jnp.sum(turned, axis=0, keepdims=True)
    stat_copy = to_sibling(dstat, dstat_in, 1)
    stat_copy.start()

    def own_block(i, carry):
        rows = pl.ds(pl.multiple_of(i * ROWS, ROWS), ROWS)
        part = dot_t(zown[0], dose[rows, 0:width])
        for j in range(1, CHUNKS):
            part = part + dot_t(zown[j], dose[rows, j * width:(j + 1) * width])
        prod[0:genes, rows] = part
        return carry

    quarter = CHUNKS // 4
    pass_on(range(quarter))
    lax.fori_loop(0, blocks // 2, own_block, 0)
    pass_on(range(quarter, 2 * quarter))
    lax.fori_loop(blocks // 2, blocks, own_block, 0)
    pass_on(range(2 * quarter, 3 * quarter))

    stat_copy.wait_recv()
    mean = (dstat[0:1, :] + dstat_in[0:1, :]) / donors
    var = (dstat[1:2, :] + dstat_in[1:2, :]) / donors - mean * mean
    rstd = lax.rsqrt(var + 1e-05)

    base = me * tiles

    def select(first, cis, sums_z, put):
        for t in range(tiles):
            cols = slice(t * TILE, (t + 1) * TILE)
            prod[first:first + genes, cols] = (
                prod[first:first + genes, cols] - mean[:, cols] * sums_z
            ) * rstd[:, cols]
        for k in range(2 * half_k):
            here = cis[:, k:k + 1] - base
            picked = jnp.zeros((genes, TILE), jnp.float32)
            for t in range(tiles):
                picked = jnp.where(
                    here == t, prod[first:first + genes, t * TILE:(t + 1) * TILE], picked
                )
            put(k // half_k, (k % half_k) * TILE, picked)

    def put_own(h, at, value):
        sel_own[h, :, at:at + TILE] = value

    select(0, cis_ref[...], z_sum, put_own)
    own_copy = to_sibling(sel_own.at[1 - core], own_in, 2)
    own_copy.start()

    pass_on(range(3 * quarter, CHUNKS))
    z_sums = jnp.zeros((2 * genes, 1), jnp.float32)
    for j in range(CHUNKS):
        @pl.when(has_far)
        def _():
            z_copy(j).wait_recv()

        both = zin[j].reshape(2 * genes, width)
        z_sums = z_sums + jnp.sum(both.astype(jnp.float32), axis=1, keepdims=True)

        def nbr_block(i, carry):
            rows = pl.ds(pl.multiple_of(i * ROWS, ROWS), ROWS)
            part = dot_t(zin[j].reshape(2 * genes, width), dose[rows, j * width:(j + 1) * width])
            if j:
                part = part + prod[genes:3 * genes, rows]
            prod[genes:3 * genes, rows] = part
            return carry

        lax.fori_loop(0, blocks, nbr_block, 0)

    for side, there, _ in sides:
        @pl.when(there)
        def _():
            cis_arrival(side).wait_recv()

        def put_nbr(h, at, value):
            sel_nbr[h, side * genes:(side + 1) * genes, at:at + TILE] = value

        select((side + 1) * genes, cin[side], z_sums[side * genes:(side + 1) * genes], put_nbr)
    nbr_copy = to_sibling(sel_nbr.at[1 - core], nbr_in, 3)
    nbr_copy.start()
    nbr_copy.wait_recv()
    ret[...] = sel_nbr[core] + nbr_in[...]
    for side, there, _ in sides:
        @pl.when(there)
        def _():
            ret_copy(side).start()

    own_copy.wait_recv()
    corr_ref[...] = sel_own[core] + own_in[...]
    for side, there, _ in sides:
        @pl.when(there)
        def _():
            ret_arrival(side).wait_recv()
            corr_ref[...] += ret_in[side]
    correlation = corr_ref[...] / donors
    corr_ref[...] = correlation
    squared = jnp.minimum(correlation * correlation, 0.9)
    shape_a = (donors - 2) / 2.0
    pval_ref[...] = tail_probability(squared, shape_a, beta_log_constant(shape_a), CF_TERMS)

    for copy in (mom_copy, stat_copy, own_copy, nbr_copy):
        copy.wait_send()
    for side, there, _ in sides:
        @pl.when(there)
        def _():
            cis_copy(side).wait_send()
            ret_copy(side).wait_send()

    for j in range(CHUNKS):
        z_copy(j).wait_send()

    @pl.when(has_ahead)
    def _():
        for j in range(CHUNKS):
            z_onward(j).wait_send()


def shards(dosage, expression, cis_tiles):
    variants, local = dosage.shape
    genes = expression.shape[0]
    cores = lax.axis_size("donor")
    regions = lax.axis_size("region")
    window = cis_tiles.shape[1]
    half = window * TILE // cores
    width = local // CHUNKS
    sizes = (genes, local, variants, regions, local * cores)
    f32, bf16 = jnp.float32, jnp.bfloat16
    dma = pltpu.SemaphoreType.DMA
    vmem = pl.BlockSpec(memory_space=pltpu.VMEM)
    hbm = pl.BlockSpec(memory_space=pltpu.HBM)
    return pl.pallas_call(
        functools.partial(kernel, sizes),
        out_shape=(
            jax.ShapeDtypeStruct((genes, half), f32),
            jax.ShapeDtypeStruct((genes, half), f32),
        ),
        in_specs=[hbm, hbm, vmem],
        out_specs=(vmem, vmem),
        scratch_shapes=[
            pltpu.VMEM((variants, local), bf16),
            pltpu.VMEM((genes, local), bf16),
            pltpu.VMEM((genes, window), jnp.int32),
            pltpu.VMEM((CHUNKS, genes, width), bf16),
            pltpu.VMEM((CHUNKS, 2, genes, width), bf16),
            pltpu.VMEM((2, genes, window), jnp.int32),
            pltpu.VMEM((genes, 128), f32),
            pltpu.VMEM((genes, 128), f32),
            pltpu.VMEM((2, variants, 128), f32),
            pltpu.VMEM((2, variants), f32),
            pltpu.VMEM((2, variants), f32),
            pltpu.VMEM((3 * genes, variants), f32),
            pltpu.VMEM((2, genes, half), f32),
            pltpu.VMEM((genes, half), f32),
            pltpu.VMEM((2, 2 * genes, half), f32),
            pltpu.VMEM((2 * genes, half), f32),
            pltpu.VMEM((2 * genes, half), f32),
            pltpu.VMEM((2, genes, half), f32),
            dma((variants // ROWS,)),
            dma,
            dma((CHUNKS,)),
            dma((CHUNKS,)),
            dma((2, CHUNKS)),
            dma((2,)),
            dma((2,)),
            dma((4,)),
            dma((4,)),
            dma((2,)),
            dma((2,)),
        ],
        compiler_params=pltpu.CompilerParams(
            collective_id=0, has_side_effects=True, vmem_limit_bytes=60 * 1024 * 1024
        ),
    )(dosage, expression, cis_tiles.T)


def solution(mesh):
    assert mesh.shape["donor"] == 2 and mesh.shape["region"] % 2 == 0
    in_specs = (
        P(("grp", "region"), "donor"),
        P(("grp", "region"), "donor"),
        P(("grp", "region"), None),
    )
    out_specs = (P(("grp", "region"), "donor"), P(("grp", "region"), "donor"))
    return jax.shard_map(shards, mesh=mesh, in_specs=in_specs, out_specs=out_specs, check_vma=False)
```

```python
import functools
import math

import jax
import jax.numpy as jnp
from jax import lax
from jax.experimental import pallas as pl
from jax.experimental.pallas import tpu as pltpu
from jax.sharding import PartitionSpec as P

TILE = 128
CF_TERMS = 32
CHUNKS = 4
ROWS = 512
MESH = pl.DeviceIdType.MESH


def beta_log_constant(shape_a):
    inverse = 1.0 / shape_a
    ratio = (
        0.5 * math.log(shape_a)
        - inverse / 8.0
        + inverse**3 / 192.0
        + inverse**5 / 640.0
        - 17.0 * inverse**7 / 14336.0
    )
    return ratio - 0.5 * math.log(math.pi)


def coefficients(a, b, terms):
    out = [-(a + b) / (a + 1.0)]
    for m in range(1, terms + 1):
        out.append(m * (b - m) / ((a + 2.0 * m - 1.0) * (a + 2.0 * m)))
        out.append(-(a + m) * (a + b + m) / ((a + 2.0 * m) * (a + 2.0 * m + 1.0)))
    return out


def tail_probability(squared, shape_a, log_const, terms):
    narrow = squared < 1.5 / (shape_a + 2.5)
    argument = jnp.where(narrow, squared, 1.0 - squared)
    small = coefficients(0.5, shape_a, terms)
    large = coefficients(shape_a, 0.5, terms)
    level = jnp.ones_like(squared)
    for c_small, c_large in zip(small[::-1], large[::-1]):
        level = 1.0 + jnp.where(narrow, c_small, c_large) * argument / level
    front = jnp.sqrt(squared) * jnp.exp(shape_a * jnp.log1p(-squared) + log_const)
    share = front / (level * jnp.where(narrow, 0.5, shape_a))
    return jnp.where(narrow, 1.0 - share, share)


def lane_sums(block_of, columns, rows):
    total = jnp.zeros((rows, 128), jnp.float32)
    square = jnp.zeros((rows, 128), jnp.float32)
    for j in range(columns // 128):
        x = block_of(j).astype(jnp.float32)
        total = total + x
        square = square + x * x
    return total, square


def dot_t(left, right):
    return lax.dot_general(
        left, right, (((1,), (1,)), ((), ())), preferred_element_type=jnp.float32
    )


def kernel(
    sizes,
    dose_hbm, expr_hbm, cis_t,
    corr_ref, pval_ref,
    dose, expr_ref, cis_ref, zown, zin, cin, mom, mom_in, acc, dstat, dstat_in, prod,
    sel_own, own_in, sel_nbr, nbr_in, ret, ret_in,
    dose_sem, expr_sem, z_send, f_send, z_recv, c_send, c_recv, s_send, s_recv, r_send, r_recv,
):
    genes, local, variants, regions, donors = sizes
    tiles = variants // TILE
    width = local // CHUNKS
    half = corr_ref.shape[1]
    half_k = half // TILE
    me = lax.axis_index("region")
    core = lax.axis_index("donor")
    has_prev = me > 0
    has_next = me < regions - 1
    prev = jnp.maximum(me - 1, 0)
    nxt = jnp.minimum(me + 1, regions - 1)
    sibling = {"donor": 1 - core}
    sides = ((0, has_prev, {"region": prev}), (1, has_next, {"region": nxt}))

    barrier = pltpu.get_barrier_semaphore()
    pl.semaphore_signal(barrier, inc=1, device_id=sibling, device_id_type=MESH)
    for _, there, where in sides:
        @pl.when(there)
        def _():
            pl.semaphore_signal(barrier, inc=1, device_id=where, device_id_type=MESH)

    odd = lax.rem(me, 2)
    far_slot, near_slot = odd, 1 - odd
    partner, ahead, behind = me + 1 - 2 * odd, me + 2 - 4 * odd, me - 2 + 4 * odd
    has_ahead = jnp.logical_and(ahead >= 0, ahead < regions)
    has_far = jnp.logical_and(behind >= 0, behind < regions)
    ahead = jnp.clip(ahead, 0, regions - 1)
    behind = jnp.clip(behind, 0, regions - 1)
    for there, where in ((has_ahead, ahead), (has_far, behind)):
        @pl.when(there)
        def _():
            pl.semaphore_signal(
                barrier, inc=1, device_id={"region": where}, device_id_type=MESH
            )

    expr_load = pltpu.make_async_copy(expr_hbm, expr_ref, expr_sem)
    expr_load.start()
    blocks = variants // ROWS
    loads = [
        pltpu.make_async_copy(
            dose_hbm.at[pl.ds(i * ROWS, ROWS)], dose.at[pl.ds(i * ROWS, ROWS)], dose_sem.at[i]
        )
        for i in range(blocks)
    ]
    for load in loads:
        load.start()

    cis_ref[...] = jnp.transpose(cis_t[...])
    expr_load.wait()
    total, square = lane_sums(lambda j: expr_ref[:, j * 128:(j + 1) * 128], local, genes)
    total = jnp.sum(total, axis=1, keepdims=True)
    square = jnp.sum(square, axis=1, keepdims=True)
    lane = lax.broadcasted_iota(jnp.int32, (genes, 128), 1)
    mom[...] = jnp.where(lane == 0, total, square)
    @pl.when(jnp.logical_not(has_far))
    def _():
        zin[:, far_slot] = jnp.zeros((CHUNKS, genes, width), jnp.bfloat16)
        cin[far_slot] = jnp.zeros(cis_ref.shape, jnp.int32)

    greeted = 1
    for there in (has_prev, has_next, has_ahead, has_far):
        greeted = greeted + there.astype(jnp.int32)
    pl.semaphore_wait(barrier, greeted)

    def to_sibling(src, dst, slot):
        return pltpu.make_async_remote_copy(
            src_ref=src, dst_ref=dst, send_sem=s_send.at[slot], recv_sem=s_recv.at[slot],
            device_id=sibling, device_id_type=MESH,
        )

    mom_copy = to_sibling(mom, mom_in, 0)
    mom_copy.start()

    def cis_copy(side):
        return pltpu.make_async_remote_copy(
            src_ref=cis_ref, dst_ref=cin.at[1 - side], send_sem=c_send.at[side],
            recv_sem=c_recv.at[1 - side], device_id=sides[side][2], device_id_type=MESH,
        )

    def z_copy(j):
        return pltpu.make_async_remote_copy(
            src_ref=zown.at[j], dst_ref=zin.at[j, far_slot], send_sem=z_send.at[j],
            recv_sem=z_recv.at[far_slot, j], device_id={"region": partner}, device_id_type=MESH,
        )

    def z_onward(j):
        return pltpu.make_async_remote_copy(
            src_ref=zin.at[j, near_slot], dst_ref=zin.at[j, far_slot], send_sem=f_send.at[j],
            recv_sem=z_recv.at[far_slot, j], device_id={"region": ahead}, device_id_type=MESH,
        )

    def z_near(j):
        return pltpu.make_async_remote_copy(
            src_ref=zown.at[j], dst_ref=zin.at[j, near_slot], send_sem=z_send.at[j],
            recv_sem=z_recv.at[near_slot, j], device_id={"region": partner}, device_id_type=MESH,
        )

    def pass_on(chunks):
        for j in chunks:
            z_near(j).wait_recv()

            @pl.when(has_ahead)
            def _():
                z_onward(j).start()

    def cis_arrival(side):
        return pltpu.make_async_remote_copy(
            src_ref=cis_ref, dst_ref=cin.at[side], send_sem=c_send.at[side],
            recv_sem=c_recv.at[side], device_id=sides[side][2], device_id_type=MESH,
        )

    def ret_copy(side):
        return pltpu.make_async_remote_copy(
            src_ref=ret.at[pl.ds(side * genes, genes)], dst_ref=ret_in.at[1 - side],
            send_sem=r_send.at[side], recv_sem=r_recv.at[1 - side],
            device_id=sides[side][2], device_id_type=MESH,
        )

    def ret_arrival(side):
        return pltpu.make_async_remote_copy(
            src_ref=ret.at[pl.ds(side * genes, genes)], dst_ref=ret_in.at[side],
            send_sem=r_send.at[side], recv_sem=r_recv.at[side],
            device_id=sides[side][2], device_id_type=MESH,
        )

    for side, there, _ in sides:
        @pl.when(there)
        def _():
            cis_copy(side).start()

    group = 32
    z_sum = jnp.zeros((genes, 1), jnp.float32)
    for i in range(blocks):
        loads[i].wait()

        def row_group(q, carry):
            start = pl.multiple_of(i * ROWS + q * group, group)
            rows = pl.ds(start, group)
            t, s = lane_sums(lambda j: dose[rows, j * 128:(j + 1) * 128], local, group)
            acc[0, rows] = t
            acc[1, rows] = s
            return carry

        lax.fori_loop(0, ROWS // group, row_group, 0)
        if i == 0:
            mom_copy.wait_recv()
            sums = mom[...] + mom_in[...]
            center = sums[:, 0:1] / donors
            spread = sums[:, 1:2] / donors - center * center
            scale = lax.rsqrt(spread + 1e-05)
            for j in range(CHUNKS):
                y = expr_ref[:, j * width:(j + 1) * width].astype(jnp.float32)
                z = ((y - center) * scale).astype(jnp.bfloat16)
                zown[j] = z
                z_copy(j).start()
                z_sum = z_sum + jnp.sum(z.astype(jnp.float32), axis=1, keepdims=True)
        for w in range(2):
            for h in range(ROWS // 128):
                at = i * ROWS + h * 128
                turned = jnp.transpose(acc[w, at:at + 128])
                dstat[w:w + 1, at:at + 128] = jnp.sum(turned, axis=0, keepdims=True)
    stat_copy = to_sibling(dstat, dstat_in, 1)
    stat_copy.start()

    def own_block(i, carry):
        rows = pl.ds(pl.multiple_of(i * ROWS, ROWS), ROWS)
        part = dot_t(zown[0], dose[rows, 0:width])
        for j in range(1, CHUNKS):
            part = part + dot_t(zown[j], dose[rows, j * width:(j + 1) * width])
        prod[0:genes, rows] = part
        return carry

    quarter = CHUNKS // 4
    pass_on(range(quarter))
    lax.fori_loop(0, blocks // 2, own_block, 0)
    pass_on(range(quarter, 2 * quarter))
    lax.fori_loop(blocks // 2, blocks, own_block, 0)
    pass_on(range(2 * quarter, 3 * quarter))

    stat_copy.wait_recv()
    mean = (dstat[0:1, :] + dstat_in[0:1, :]) / donors
    var = (dstat[1:2, :] + dstat_in[1:2, :]) / donors - mean * mean
    rstd = lax.rsqrt(var + 1e-05)

    base = me * tiles

    def select(first, cis, sums_z, put):
        for t in range(tiles):
            cols = slice(t * TILE, (t + 1) * TILE)
            prod[first:first + genes, cols] = (
                prod[first:first + genes, cols] - mean[:, cols] * sums_z
            ) * rstd[:, cols]
        for k in range(2 * half_k):
            here = cis[:, k:k + 1] - base
            picked = jnp.zeros((genes, TILE), jnp.float32)
            for t in range(tiles):
                picked = jnp.where(
                    here == t, prod[first:first + genes, t * TILE:(t + 1) * TILE], picked
                )
            put(k // half_k, (k % half_k) * TILE, picked)

    def put_own(h, at, value):
        sel_own[h, :, at:at + TILE] = value

    select(0, cis_ref[...], z_sum, put_own)
    own_copy = to_sibling(sel_own.at[1 - core], own_in, 2)
    own_copy.start()

    pass_on(range(3 * quarter, CHUNKS))
    z_sums = jnp.zeros((2 * genes, 1), jnp.float32)
    for j in range(CHUNKS):
        @pl.when(has_far)
        def _():
            z_copy(j).wait_recv()

        both = zin[j].reshape(2 * genes, width)
        z_sums = z_sums + jnp.sum(both.astype(jnp.float32), axis=1, keepdims=True)

        def nbr_block(i, carry):
            rows = pl.ds(pl.multiple_of(i * ROWS, ROWS), ROWS)
            part = dot_t(zin[j].reshape(2 * genes, width), dose[rows, j * width:(j + 1) * width])
            if j:
                part = part + prod[genes:3 * genes, rows]
            prod[genes:3 * genes, rows] = part
            return carry

        lax.fori_loop(0, blocks, nbr_block, 0)

    for side, there, _ in sides:
        @pl.when(there)
        def _():
            cis_arrival(side).wait_recv()

        def put_nbr(h, at, value):
            sel_nbr[h, side * genes:(side + 1) * genes, at:at + TILE] = value

        select((side + 1) * genes, cin[side], z_sums[side * genes:(side + 1) * genes], put_nbr)
    nbr_copy = to_sibling(sel_nbr.at[1 - core], nbr_in, 3)
    nbr_copy.start()
    nbr_copy.wait_recv()
    ret[...] = sel_nbr[core] + nbr_in[...]
    for side, there, _ in sides:
        @pl.when(there)
        def _():
            ret_copy(side).start()

    own_copy.wait_recv()
    corr_ref[...] = sel_own[core] + own_in[...]
    for side, there, _ in sides:
        @pl.when(there)
        def _():
            ret_arrival(side).wait_recv()
            corr_ref[...] += ret_in[side]
    correlation = corr_ref[...] / donors
    corr_ref[...] = correlation
    squared = jnp.minimum(correlation * correlation, 0.9)
    shape_a = (donors - 2) / 2.0
    pval_ref[...] = tail_probability(squared, shape_a, beta_log_constant(shape_a), CF_TERMS)

    for copy in (mom_copy, stat_copy, own_copy, nbr_copy):
        copy.wait_send()
    for side, there, _ in sides:
        @pl.when(there)
        def _():
            cis_copy(side).wait_send()
            ret_copy(side).wait_send()

    for j in range(CHUNKS):
        z_copy(j).wait_send()

    @pl.when(has_ahead)
    def _():
        for j in range(CHUNKS):
            z_onward(j).wait_send()


def shards(dosage, expression, cis_tiles):
    variants, local = dosage.shape
    genes = expression.shape[0]
    cores = lax.axis_size("donor")
    regions = lax.axis_size("region")
    window = cis_tiles.shape[1]
    half = window * TILE // cores
    width = local // CHUNKS
    sizes = (genes, local, variants, regions, local * cores)
    f32, bf16 = jnp.float32, jnp.bfloat16
    dma = pltpu.SemaphoreType.DMA
    vmem = pl.BlockSpec(memory_space=pltpu.VMEM)
    hbm = pl.BlockSpec(memory_space=pltpu.HBM)
    return pl.pallas_call(
        functools.partial(kernel, sizes),
        out_shape=(
            jax.ShapeDtypeStruct((genes, half), f32),
            jax.ShapeDtypeStruct((genes, half), f32),
        ),
        in_specs=[hbm, hbm, vmem],
        out_specs=(vmem, vmem),
        scratch_shapes=[
            pltpu.VMEM((variants, local), bf16),
            pltpu.VMEM((genes, local), bf16),
            pltpu.VMEM((genes, window), jnp.int32),
            pltpu.VMEM((CHUNKS, genes, width), bf16),
            pltpu.VMEM((CHUNKS, 2, genes, width), bf16),
            pltpu.VMEM((2, genes, window), jnp.int32),
            pltpu.VMEM((genes, 128), f32),
            pltpu.VMEM((genes, 128), f32),
            pltpu.VMEM((2, variants, 128), f32),
            pltpu.VMEM((2, variants), f32),
            pltpu.VMEM((2, variants), f32),
            pltpu.VMEM((3 * genes, variants), f32),
            pltpu.VMEM((2, genes, half), f32),
            pltpu.VMEM((genes, half), f32),
            pltpu.VMEM((2, 2 * genes, half), f32),
            pltpu.VMEM((2 * genes, half), f32),
            pltpu.VMEM((2 * genes, half), f32),
            pltpu.VMEM((2, genes, half), f32),
            dma((variants // ROWS,)),
            dma,
            dma((CHUNKS,)),
            dma((CHUNKS,)),
            dma((2, CHUNKS)),
            dma((2,)),
            dma((2,)),
            dma((4,)),
            dma((4,)),
            dma((2,)),
            dma((2,)),
        ],
        compiler_params=pltpu.CompilerParams(
            collective_id=0, has_side_effects=True, vmem_limit_bytes=60 * 1024 * 1024
        ),
    )(dosage, expression, cis_tiles.T)


def solution(mesh):
    assert mesh.shape["donor"] == 2 and mesh.shape["region"] % 2 == 0
    in_specs = (
        P(("grp", "region"), "donor"),
        P(("grp", "region"), "donor"),
        P(("grp", "region"), None),
    )
    out_specs = (P(("grp", "region"), "donor"), P(("grp", "region"), "donor"))
    return jax.shard_map(shards, mesh=mesh, in_specs=in_specs, out_specs=out_specs, check_vma=False)
```
